32 devices in a mesh: groups: 2 (over x), samples: 16 (over z, y, core).
Axes of the slice: x: 2, y: 2, z: 4, core: 2. Of those that a mesh axis runs over, the one named last changes fastest.
Arguments:
- terms: float32 [1048576, 64], P(('groups', 'samples')), parts along dimension 0
- coefficients: float32 [64, 256], replicated, may hold values from -1.5 to 1.5
- counts: int32 [512], P('groups'), parts along dimension 0, may hold values from 1 to 4095, as said below
- labels: int32 [1048576], P(('groups', 'samples')), parts along dimension 0, may hold values from 0 to 255, as said below
- f_start: float32 [512], P('groups'), parts along dimension 0, may hold values from -8 to 8
Outputs:
- free: float32 [512], P('groups'), parts along dimension 0
- intersection: float32 [512, 256], P(('groups', 'samples')), parts along dimension 0
- anchor_mix: float32 [512, 256], P(('groups', 'samples')), parts along dimension 0
- term_means: float32 [512, 64], P(('groups', 'samples')), parts along dimension 0
The draws below stay inside these ranges and needn't reach their ends.
There are 2 independent parts, one for each index of `groups`. The reference program is written for one: setup_inputs(seed, part) draws one part's arguments, and reference() takes and returns one part's arrays. A program takes and returns all parts, laid end to end along the dimension named above; an argument that names none is the same for every part. Nothing has to cross between parts.
Inputs may be any that keep to these rules, and one draw needn't show every extreme that they name: counts sum to 524288. `labels`: exactly counts[k] snapshots carry the label k.
All inputs are finite; a program needn't handle non-finite values.
Results may differ from the reference program's by a relative error of at most 0.0003.
Values sent between devices are 32-bit elements; how exact they have to be, the bound alone decides.
A program may use at most 128 MiB of HBM per device.

```python
import jax
import jax.numpy as jnp
from jax import lax

STATES = 256
TERMS = 64
ITERS = 4
ROWS_DEV = 32768
SNAPSHOTS = 524288


def counts_helper(key):
    base = SNAPSHOTS // STATES
    extra = jax.random.randint(jax.random.fold_in(key, 11), (STATES,), 0, base)
    extra = extra.at[0].set(base - 1).at[1].set(0).at[STATES - 1].set(0)
    return base + extra - jnp.roll(extra, 1)


def draw_counts(key, part):
    return counts_helper(key).astype(jnp.int32)


def draw_labels(key, part):
    counts = counts_helper(key)
    bounds = jnp.cumsum(counts)
    positions = jnp.arange(SNAPSHOTS, dtype=jnp.int32)
    ordered = jnp.searchsorted(bounds, positions, side='right').astype(jnp.int32)
    order = jax.random.permutation(jax.random.fold_in(key, 13), SNAPSHOTS)
    return ordered[order].astype(jnp.int32)


def draw_terms(key, part):
    first = jax.random.fold_in(key, 21)
    second = jax.random.fold_in(key, 22)
    row_scale = jnp.exp(jax.random.uniform(second, (SNAPSHOTS, 1), jnp.float32, 0.0, 2.3)) * 0.4
    values = jax.random.normal(first, (SNAPSHOTS, TERMS), jnp.float32)
    return jnp.clip(values, -6.0, 6.0) * row_scale


def bell_draw(own_key, shape, scale, most, kind=jnp.bfloat16):
    result = scale * jax.random.normal(own_key, shape, jnp.float32)
    return jnp.clip(result, min=-most, max=most).astype(kind)


def setup_inputs(seed: int = 0, part: int = 0) -> dict:
    splits = jax.random.split(jax.random.key(seed), 6)
    part_splits = jax.random.split(jax.random.fold_in(splits[5], part), 6)
    return {
        "terms": draw_terms(jax.random.fold_in(jax.random.fold_in(splits[5], part), 71), part),
        "coefficients": bell_draw(splits[1], (TERMS, STATES), (TERMS // 4) ** -0.5, 1.5, jnp.float32),
        "counts": draw_counts(jax.random.fold_in(jax.random.fold_in(splits[5], part), 71), part),
        "labels": draw_labels(jax.random.fold_in(jax.random.fold_in(splits[5], part), 71), part),
        "f_start": bell_draw(part_splits[4], (STATES,), 2.0, 8.0, jnp.float32),
    }


def energies(block, coefficients):
    return jnp.dot(block, coefficients, precision=lax.Precision.HIGHEST, preferred_element_type=jnp.float32)


def denominator(energy, free_now, log_counts):
    shifted = log_counts[None, :] + free_now[None, :] - energy
    top = jnp.max(shifted, axis=1, keepdims=True)
    return top[:, 0] + jnp.log(jnp.sum(jnp.exp(shifted - top), axis=1))


def reference(terms, coefficients, counts, labels, f_start):
    block_rows = min(4096, ROWS_DEV)
    blocks = terms.reshape(-1, block_rows, TERMS)
    label_blocks = labels.reshape(-1, block_rows)
    log_counts = jnp.log(counts.astype(jnp.float32))
    scaled_counts = counts.astype(jnp.float32)
    free_now = f_start

    for step in range(ITERS):
        def accumulate(carry, block):
            peak, total = carry
            energy = energies(block, coefficients)
            denom = denominator(energy, free_now, log_counts)
            logw = -energy - denom[:, None]
            new_peak = jnp.maximum(peak, jnp.max(logw, axis=0))
            total = total * jnp.exp(peak - new_peak) + jnp.sum(jnp.exp(logw - new_peak[None, :]), axis=0)
            return (new_peak, total), None

        init = (jnp.full((STATES,), -1e30, jnp.float32), jnp.zeros((STATES,), jnp.float32))
        (peak, total), _ = lax.scan(accumulate, init, blocks)
        updated = -(peak + jnp.log(total))
        free_now = updated - updated[0]

    state_ids = jnp.arange(STATES, dtype=jnp.int32)

    def diagnose(carry, pair):
        over, anchor, term_sum, weight_sum = carry
        block, label_block = pair
        energy = energies(block, coefficients)
        denom = denominator(energy, free_now, log_counts)
        weight = jnp.exp(free_now[None, :] - energy - denom[:, None])
        over = over + jnp.dot(weight.T, weight * scaled_counts[None, :], precision=lax.Precision.HIGHEST, preferred_element_type=jnp.float32)
        onehot = (label_block[:, None] == state_ids[None, :]).astype(jnp.float32)
        anchor = anchor + jnp.dot(onehot.T, weight, precision=lax.Precision.HIGHEST, preferred_element_type=jnp.float32)
        term_sum = term_sum + jnp.dot(weight.T, block, precision=lax.Precision.HIGHEST, preferred_element_type=jnp.float32)
        weight_sum = weight_sum + jnp.sum(weight, axis=0)
        return (over, anchor, term_sum, weight_sum), None

    init = (jnp.zeros((STATES, STATES), jnp.float32), jnp.zeros((STATES, STATES), jnp.float32),
            jnp.zeros((STATES, TERMS), jnp.float32), jnp.zeros((STATES,), jnp.float32))
    (over, anchor, term_sum, weight_sum), _ = lax.scan(diagnose, init, (blocks, label_blocks))
    return free_now, over, anchor, term_sum / weight_sum[:, None]
```

```python
import functools

import jax
import jax.numpy as jnp
from jax import lax
from jax.experimental import pallas as pl
from jax.experimental.pallas import tpu as pltpu
from jax.sharding import PartitionSpec as P

ITERS = 4


def energies(block, coefficients):
    return jnp.dot(
        block, coefficients, precision=lax.Precision.HIGHEST, preferred_element_type=jnp.float32
    )


def denominator(energy, free_now, log_counts):
    shifted = log_counts[None, :] + free_now[None, :] - energy
    top = jnp.max(shifted, axis=1, keepdims=True)
    return top[:, 0] + jnp.log(jnp.sum(jnp.exp(shifted - top), axis=1))


def general(terms, coefficients, counts, labels, f_start):
    rows = terms.shape[0]
    states = coefficients.shape[1]
    block_rows = min(4096, rows)
    blocks = terms.reshape(rows // block_rows, block_rows, terms.shape[1])
    label_blocks = labels.reshape(rows // block_rows, block_rows)
    log_counts = jnp.log(counts.astype(jnp.float32))
    scaled_counts = counts.astype(jnp.float32)
    free_now = f_start
    for step in range(ITERS):

        def accumulate(carry, block):
            peak, total = carry
            energy = energies(block, coefficients)
            denom = denominator(energy, free_now, log_counts)
            logw = -energy - denom[:, None]
            new_peak = jnp.maximum(peak, jnp.max(logw, axis=0))
            total = total * jnp.exp(peak - new_peak) + jnp.sum(
                jnp.exp(logw - new_peak[None, :]), axis=0
            )
            return ((new_peak, total), None)

        init = (jnp.full((states,), -1e30, jnp.float32), jnp.zeros((states,), jnp.float32))
        (peak, total), _ = lax.scan(accumulate, init, blocks)
        highest = lax.pmax(peak, "samples")
        total = lax.psum(total * jnp.exp(peak - highest), "samples")
        peak = highest
        updated = -(peak + jnp.log(total))
        free_now = updated - updated[0]
    state_ids = jnp.arange(states, dtype=jnp.int32)

    def diagnose(carry, pair):
        over, anchor, term_sum, weight_sum = carry
        block, label_block = pair
        energy = energies(block, coefficients)
        denom = denominator(energy, free_now, log_counts)
        weight = jnp.exp(free_now[None, :] - energy - denom[:, None])
        over = over + jnp.dot(
            weight.T,
            weight * scaled_counts[None, :],
            precision=lax.Precision.HIGHEST,
            preferred_element_type=jnp.float32,
        )
        onehot = (label_block[:, None] == state_ids[None, :]).astype(jnp.float32)
        anchor = anchor + jnp.dot(
            onehot.T, weight, precision=lax.Precision.HIGHEST, preferred_element_type=jnp.float32
        )
        term_sum = term_sum + jnp.dot(
            weight.T, block, precision=lax.Precision.HIGHEST, preferred_element_type=jnp.float32
        )
        weight_sum = weight_sum + jnp.sum(weight, axis=0)
        return ((over, anchor, term_sum, weight_sum), None)

    init = (
        jnp.zeros((states, states), jnp.float32),
        jnp.zeros((states, states), jnp.float32),
        jnp.zeros((states, terms.shape[1]), jnp.float32),
        jnp.zeros((states,), jnp.float32),
    )
    (over, anchor, term_sum, weight_sum), _ = lax.scan(diagnose, init, (blocks, label_blocks))
    over, anchor, term_sum, weight_sum = lax.psum((over, anchor, term_sum, weight_sum), "samples")
    owned = states // lax.axis_size("samples")
    first_row = lax.axis_index("samples") * owned
    over = lax.dynamic_slice_in_dim(over, first_row, owned, 0)
    anchor = lax.dynamic_slice_in_dim(anchor, first_row, owned, 0)
    term_sum = lax.dynamic_slice_in_dim(term_sum, first_row, owned, 0)
    weight_sum = lax.dynamic_slice_in_dim(weight_sum, first_row, owned, 0)
    return (free_now, over, anchor, term_sum / weight_sum[:, None])


LOG2E = 1.4426950408889634
LIFT = 57.0
MESH = pl.DeviceIdType.MESH


def lanes_to_column(rows_form):
    parts = [
        jnp.broadcast_to(rows_form[r : r + 1, :], (128, 128)).T for r in range(rows_form.shape[0])
    ]
    return jnp.concatenate(parts, axis=0)


def split(x):
    high = x.astype(jnp.bfloat16)
    rest = x - high.astype(jnp.float32)
    middle = rest.astype(jnp.bfloat16)
    low = (rest - middle.astype(jnp.float32)).astype(jnp.bfloat16)
    return high, middle, low


def mbar_kernel(
    n,
    groups,
    terms_ref,
    coef_ref,
    counts_ref,
    labels_ref,
    start_ref,
    free_ref,
    over_ref,
    anchor_ref,
    means_ref,
    ok_ref,
    q_ref,
    t_ref,
    a_ref,
    w_ref,
    d_ref,
    acc_ref,
    inv_ref,
    x_ref,
    left_ref,
    right_ref,
    comm_ref,
    flag_ref,
    big_ref,
    half_ref,
    red_ref,
    got_ref,
    load_sem,
    send_sem,
    recv_sem,
    flag_send,
    flag_recv,
    half_sem,
    out_send,
    out_recv,
):
    f32, bf16 = jnp.float32, jnp.bfloat16
    group = lax.axis_index("groups")
    me = lax.axis_index("samples")
    states = q_ref.shape[0]
    rows = q_ref.shape[1]
    terms = t_ref.shape[0]
    owned = states // n
    chunks = load_sem.shape[0]
    chunk = rows // chunks

    def load(c):
        cols = pl.ds(pl.multiple_of(c * chunk, chunk), chunk)
        return pltpu.make_async_copy(terms_ref.at[:, cols], t_ref.at[:, cols], load_sem.at[c])

    barrier = pltpu.get_barrier_semaphore()
    for d in range(1, n):
        pl.semaphore_signal(
            barrier, inc=1, device_id=(group, lax.rem(me + d, n)), device_id_type=MESH
        )
    for d in range(1, groups):
        pl.semaphore_signal(
            barrier, inc=1, device_id=(lax.rem(group + d, groups), me), device_id_type=MESH
        )
    for c in range(chunks):
        load(c).start()

    ch, cm, cl = (p.astype(f32) for p in split(coef_ref[...] * (-LOG2E)))
    a_ref[...] = jnp.concatenate([ch, ch, cm, cm, ch, cl], axis=0).T.astype(bf16)

    counts = counts_ref[...].astype(f32)
    log_counts = jnp.log(counts)
    tiny = 1e-15
    most = 1e10

    def state_weights(free):
        shifted = log_counts + free
        top = jnp.max(jnp.max(shifted, axis=1, keepdims=True), axis=0, keepdims=True)
        return jnp.exp(shifted - top), top

    def gather_sums(cols, width):
        s = None
        for k in range(0, states, 8):
            w = w_ref[k : k + 8, :]
            p = [q_ref[k : k + 8, pl.ds(cols + j, 128)] * w for j in range(0, width, 128)]
            s = p if s is None else [x + y for x, y in zip(s, p)]
        inv = [1.0 / jnp.sum(x, axis=0, keepdims=True) for x in s]
        peak = functools.reduce(jnp.maximum, inv)
        inv_ref[...] = jnp.maximum(inv_ref[...], peak)
        wide = [jnp.broadcast_to(x, (8, 128)) for x in inv]
        for k in range(0, states, 8):
            t = [
                q_ref[k : k + 8, pl.ds(cols + j, 128)] * wide[i]
                for i, j in enumerate(range(0, width, 128))
            ]
            while len(t) > 1:
                t = [t[i] + t[i + 1] for i in range(0, len(t), 2)]
            acc_ref[k : k + 8, :] += t[0]

    def clear():
        acc_ref[...] = jnp.zeros_like(acc_ref)
        inv_ref[...] = jnp.zeros_like(inv_ref)

    weights, _ = state_weights(start_ref[...])
    w_ref[...] = lanes_to_column(weights)
    clear()

    wa = WIDTH_A
    wi = WIDTH_I

    def energy_block(b, carry):
        cols = pl.multiple_of(b * wa, wa)
        th, tm, tl = split(t_ref[:, pl.ds(cols, wa)])
        stacked = jnp.concatenate([th, tm, th, tm, tl, th], axis=0)
        e = jnp.dot(a_ref[...], stacked, preferred_element_type=f32)
        top = jnp.max(e, axis=0, keepdims=True) - LIFT
        q_ref[:, pl.ds(cols, wa)] = jnp.exp2(e - top)
        gather_sums(cols, wa)
        return carry

    def energy_chunk(c, carry):
        load(c).wait()
        per = chunk // wa
        lax.fori_loop(c * per, (c + 1) * per, energy_block, 0)
        return carry

    lax.fori_loop(0, chunks, energy_chunk, 0)
    pl.semaphore_wait(barrier, n - 1 + groups - 1)

    good = counts > 0.0
    free = None
    for it in range(ITERS):
        if it:
            clear()

            def pass_block(b, carry):
                gather_sums(pl.multiple_of(b * wi, wi), wi)
                return carry

            lax.fori_loop(0, rows // wi, pass_block, 0)
        sums = jnp.sum(acc_ref[...].T, axis=0, keepdims=True)
        halves = [sums[:, r : r + 128] for r in range(0, states, 128)]
        pad = comm_ref.shape[2] - len(halves)
        comm_ref[it, me] = jnp.concatenate(halves + [inv_ref[...]] * pad, axis=0)
        copies = []
        for d in range(1, n):
            copy = pltpu.make_async_remote_copy(
                src_ref=comm_ref.at[it, me],
                dst_ref=comm_ref.at[it, me],
                send_sem=send_sem.at[it, d],
                recv_sem=recv_sem.at[it, d],
                device_id=(group, lax.rem(me + d, n)),
                device_id_type=MESH,
            )
            copy.start()
            copies.append(copy)
        for copy in copies:
            copy.wait()
        everyone = comm_ref[it]
        total = jnp.sum(everyone[:, : states // 128], axis=0)
        peak = jnp.max(jnp.max(everyone, axis=0)[states // 128 :], axis=0, keepdims=True)
        peak = jnp.max(peak, axis=1, keepdims=True)
        good = good & (total >= tiny) & (peak <= most)
        logs = jnp.log(total)
        free = logs[0:1, 0:1] - logs
        before = weights
        weights, top = state_weights(free)
        w_ref[...] = lanes_to_column(weights)
    free_ref[...] = free

    change = weights / before
    least = jnp.min(jnp.min(change, axis=1, keepdims=True), axis=0, keepdims=True)
    widest = jnp.max(jnp.max(change, axis=1, keepdims=True), axis=0, keepdims=True)
    good = good & (weights >= 1e-30) & (peak <= most * least) & (total >= tiny * widest)
    good = jnp.min(jnp.where(good, 1.0, 0.0), axis=0, keepdims=True)
    good = jnp.broadcast_to(jnp.min(good, axis=1, keepdims=True), (8, 128))
    flag_ref[group] = good
    flags = []
    for d in range(1, groups):
        copy = pltpu.make_async_remote_copy(
            src_ref=flag_ref.at[group],
            dst_ref=flag_ref.at[group],
            send_sem=flag_send.at[d],
            recv_sem=flag_recv.at[d],
            device_id=(lax.rem(group + d, groups), me),
            device_id_type=MESH,
        )
        copy.start()
        flags.append(copy)

    d_ref[...] = lanes_to_column(jnp.exp(free - top))
    left_ref[...] = jnp.zeros_like(left_ref)
    right_ref[...] = jnp.zeros_like(right_ref)
    wd = x_ref.shape[1]
    sub = 512
    base = 3 * states
    x_ref[base + terms : base + terms + 16, :] = jnp.ones((16, wd), bf16)

    def weights_block(b, carry):
        cols = pl.multiple_of(b * wd, wd)
        for o in range(0, wd, sub):
            s = None
            for k in range(0, states, 8):
                w = w_ref[k : k + 8, :]
                p = [q_ref[k : k + 8, pl.ds(cols + o + j, 128)] * w for j in range(0, sub, 128)]
                s = p if s is None else [x + y for x, y in zip(s, p)]
            inv = [1.0 / jnp.sum(x, axis=0, keepdims=True) for x in s]
            wide = [jnp.broadcast_to(x, (16, 128)) for x in inv]
            names = [
                jnp.broadcast_to(labels_ref[:, pl.ds(cols + o + j, 128)], (16, 128))
                for j in range(0, sub, 128)
            ]
            ids = lax.broadcasted_iota(jnp.int32, (16, 128), 0)
            for k in range(0, states, 16):
                scale = d_ref[k : k + 16, :]
                for i, j in enumerate(range(0, sub, 128)):
                    v = q_ref[k : k + 16, pl.ds(cols + o + j, 128)] * wide[i] * scale
                    high = v.astype(bf16)
                    x_ref[k : k + 16, o + j : o + j + 128] = high
                    x_ref[states + k : states + k + 16, o + j : o + j + 128] = (
                        v - high.astype(f32)
                    ).astype(bf16)
                    x_ref[2 * states + k : 2 * states + k + 16, o + j : o + j + 128] = jnp.where(
                        names[i] == ids + k, 1.0, 0.0
                    ).astype(bf16)
            t = t_ref[:, pl.ds(cols + o, sub)]
            th = t.astype(bf16)
            x_ref[base : base + terms, o : o + sub] = th
            x_ref[base + terms + 16 : base + 2 * terms + 16, o : o + sub] = (
                t - th.astype(f32)
            ).astype(bf16)
        nt = (((1,), (1,)), ((), ()))
        left_ref[...] += lax.dot_general(
            x_ref[...], x_ref[0:states, :], nt, preferred_element_type=f32
        )
        right_ref[...] += lax.dot_general(
            x_ref[2 * states : base + terms + 16, :],
            x_ref[states : 2 * states, :],
            nt,
            preferred_element_type=f32,
        )
        return carry

    lax.fori_loop(0, rows // wd, weights_block, 0)

    cross = left_ref[states : 2 * states, :]
    over = left_ref[0:states, :] + cross + cross.T
    anchor = left_ref[2 * states : base, :] + right_ref[0:states, :]
    sums = (
        left_ref[base : base + terms, :]
        + left_ref[base + terms + 16 : base + 2 * terms + 16, :]
        + right_ref[states : states + terms, :]
    )
    mass = left_ref[base + terms : base + terms + 16, :] + right_ref[
        states + terms : states + terms + 16, :
    ]
    fill = jnp.zeros((128 - terms - 16, states), f32)
    sums = jnp.concatenate([sums, mass, fill], axis=0).T
    for p in range(n):
        own = slice(p * owned, (p + 1) * owned)
        big_ref[p % 2, p // 2, :, 0:states] = over[own]
        big_ref[p % 2, p // 2, :, states : 2 * states] = anchor[own]
        big_ref[p % 2, p // 2, :, 2 * states :] = sums[own]

    side = lax.rem(me, 2)
    place = me // 2
    pair = pltpu.make_async_remote_copy(
        src_ref=big_ref.at[1 - side],
        dst_ref=half_ref,
        send_sem=half_sem.at[0],
        recv_sem=half_sem.at[1],
        device_id=(group, place * 2 + 1 - side),
        device_id_type=MESH,
    )
    pair.start()
    pair.wait()
    red_ref[...] = big_ref[side] + half_ref[...]
    copies = []
    for d in range(1, n // 2):
        there = lax.rem(place + d, n // 2)
        copy = pltpu.make_async_remote_copy(
            src_ref=red_ref.at[there],
            dst_ref=got_ref.at[place],
            send_sem=out_send.at[d],
            recv_sem=out_recv.at[d],
            device_id=(group, there * 2 + side),
            device_id_type=MESH,
        )
        copy.start()
        copies.append(copy)
    got_ref[place] = red_ref[place]
    for copy in copies:
        copy.wait()
    for copy in flags:
        copy.wait()
    ok_ref[...] = jnp.min(flag_ref[...], axis=0)
    final = jnp.sum(got_ref[...], axis=0)
    wide_counts = jnp.concatenate([counts[r : r + 1] for r in range(states // 128)], axis=1)
    over_ref[...] = final[:, 0:states] * wide_counts
    anchor_ref[...] = final[:, states : 2 * states]
    tail = final[:, 2 * states :]
    means_ref[...] = tail[:, 0:terms] / tail[:, terms : terms + 1]


WIDTH_A = 512
WIDTH_I = 1024
WIDTH_D = 2048


def local(n, groups, terms, coefficients, counts, labels, f_start):
    rows, width = terms.shape
    states = coefficients.shape[1]
    f32, bf16 = jnp.float32, jnp.bfloat16
    owned = states // n
    chunks = 8
    vmem = pl.BlockSpec(memory_space=pltpu.VMEM)
    stacked = 3 * states + 2 * width + 16
    block = (n // 2, owned, 2 * states + 128)
    dma = pltpu.SemaphoreType.DMA
    free, over, anchor, means, ok = pl.pallas_call(
        functools.partial(mbar_kernel, n, groups),
        out_shape=(
            jax.ShapeDtypeStruct((states // 128, 128), f32),
            jax.ShapeDtypeStruct((owned, states), f32),
            jax.ShapeDtypeStruct((owned, states), f32),
            jax.ShapeDtypeStruct((owned, width), f32),
            jax.ShapeDtypeStruct((8, 128), f32),
        ),
        in_specs=[pl.BlockSpec(memory_space=pltpu.HBM), vmem, vmem, vmem, vmem],
        out_specs=(vmem,) * 5,
        scratch_shapes=[
            pltpu.VMEM((states, rows), f32),
            pltpu.VMEM((width, rows), f32),
            pltpu.VMEM((states, 6 * width), bf16),
            pltpu.VMEM((states, 128), f32),
            pltpu.VMEM((states, 128), f32),
            pltpu.VMEM((states, 128), f32),
            pltpu.VMEM((1, 128), f32),
            pltpu.VMEM((stacked, WIDTH_D), bf16),
            pltpu.VMEM((stacked, states), f32),
            pltpu.VMEM((states + width + 16, states), f32),
            pltpu.VMEM((ITERS, n, 4, 128), f32),
            pltpu.VMEM((groups, 8, 128), f32),
            pltpu.VMEM((2,) + block, f32),
            pltpu.VMEM(block, f32),
            pltpu.VMEM(block, f32),
            pltpu.VMEM(block, f32),
            dma((chunks,)),
            dma((ITERS, n)),
            dma((ITERS, n)),
            dma((groups,)),
            dma((groups,)),
            dma((2,)),
            dma((n // 2,)),
            dma((n // 2,)),
        ],
        compiler_params=pltpu.CompilerParams(
            collective_id=0, has_side_effects=True, vmem_limit_bytes=62 * 1024 * 1024
        ),
    )(
        terms.T,
        coefficients,
        counts.reshape(states // 128, 128),
        labels.reshape(1, rows),
        f_start.reshape(states // 128, 128),
    )
    fast = (free.reshape(states), over, anchor, means)
    return lax.cond(
        ok[0, 0] > 0.5,
        lambda: fast,
        lambda: general(terms, coefficients, counts, labels, f_start),
    )


def solution(mesh):
    return jax.shard_map(
        functools.partial(local, mesh.shape["samples"], mesh.shape["groups"]),
        mesh=mesh,
        in_specs=(
            P(("groups", "samples"), None),
            P(),
            P("groups"),
            P(("groups", "samples")),
            P("groups"),
        ),
        out_specs=(
            P("groups"),
            P(("groups", "samples"), None),
            P(("groups", "samples"), None),
            P(("groups", "samples"), None),
        ),
        check_vma=False,
    )
```

```python
import functools

import jax
import jax.numpy as jnp
from jax import lax
from jax.experimental import pallas as pl
from jax.experimental.pallas import tpu as pltpu
from jax.sharding import PartitionSpec as P

ITERS = 4


def energies(block, coefficients):
    return jnp.dot(
        block, coefficients, precision=lax.Precision.HIGHEST, preferred_element_type=jnp.float32
    )


def denominator(energy, free_now, log_counts):
    shifted = log_counts[None, :] + free_now[None, :] - energy
    top = jnp.max(shifted, axis=1, keepdims=True)
    return top[:, 0] + jnp.log(jnp.sum(jnp.exp(shifted - top), axis=1))


def from_all(x):
    n = lax.axis_size("samples")
    me = lax.axis_index("samples")
    ring = [(i, (i + 1) % n) for i in range(n)]

    def step(d, carry):
        moving, held = carry
        moving = lax.ppermute(moving, "samples", ring)
        return moving, lax.dynamic_update_index_in_dim(held, moving, lax.rem(me - d + n, n), 0)

    held = lax.dynamic_update_index_in_dim(jnp.zeros((n,) + x.shape, x.dtype), x, me, 0)
    return lax.fori_loop(1, n, step, (x, held))[1]


def general(terms, coefficients, counts, labels, f_start):
    rows = terms.shape[0]
    states = coefficients.shape[1]
    block_rows = min(4096, rows)
    blocks = terms.reshape(rows // block_rows, block_rows, terms.shape[1])
    label_blocks = labels.reshape(rows // block_rows, block_rows)
    log_counts = jnp.log(counts.astype(jnp.float32))
    scaled_counts = counts.astype(jnp.float32)
    def iterate(step, free_now):

        def accumulate(carry, block):
            peak, total = carry
            energy = energies(block, coefficients)
            denom = denominator(energy, free_now, log_counts)
            logw = -energy - denom[:, None]
            new_peak = jnp.maximum(peak, jnp.max(logw, axis=0))
            total = total * jnp.exp(peak - new_peak) + jnp.sum(
                jnp.exp(logw - new_peak[None, :]), axis=0
            )
            return ((new_peak, total), None)

        init = (jnp.full((states,), -1e30, jnp.float32), jnp.zeros((states,), jnp.float32))
        (peak, total), _ = lax.scan(accumulate, init, blocks)
        highest = jnp.max(from_all(peak), axis=0)
        total = jnp.sum(from_all(total * jnp.exp(peak - highest)), axis=0)
        peak = highest
        updated = -(peak + jnp.log(total))
        return updated - updated[0]

    free_now = lax.fori_loop(0, ITERS, iterate, f_start)
    state_ids = jnp.arange(states, dtype=jnp.int32)

    def diagnose(carry, pair):
        over, anchor, term_sum, weight_sum = carry
        block, label_block = pair
        energy = energies(block, coefficients)
        denom = denominator(energy, free_now, log_counts)
        weight = jnp.exp(free_now[None, :] - energy - denom[:, None])
        over = over + jnp.dot(
            weight.T,
            weight * scaled_counts[None, :],
            precision=lax.Precision.HIGHEST,
            preferred_element_type=jnp.float32,
        )
        onehot = (label_block[:, None] == state_ids[None, :]).astype(jnp.float32)
        anchor = anchor + jnp.dot(
            onehot.T, weight, precision=lax.Precision.HIGHEST, preferred_element_type=jnp.float32
        )
        term_sum = term_sum + jnp.dot(
            weight.T, block, precision=lax.Precision.HIGHEST, preferred_element_type=jnp.float32
        )
        weight_sum = weight_sum + jnp.sum(weight, axis=0)
        return ((over, anchor, term_sum, weight_sum), None)

    init = (
        jnp.zeros((states, states), jnp.float32),
        jnp.zeros((states, states), jnp.float32),
        jnp.zeros((states, terms.shape[1]), jnp.float32),
        jnp.zeros((states,), jnp.float32),
    )
    (over, anchor, term_sum, weight_sum), _ = lax.scan(diagnose, init, (blocks, label_blocks))
    over, anchor, term_sum, weight_sum = (
        jnp.sum(from_all(x), axis=0) for x in (over, anchor, term_sum, weight_sum)
    )
    owned = states // lax.axis_size("samples")
    first_row = lax.axis_index("samples") * owned
    over = lax.dynamic_slice_in_dim(over, first_row, owned, 0)
    anchor = lax.dynamic_slice_in_dim(anchor, first_row, owned, 0)
    term_sum = lax.dynamic_slice_in_dim(term_sum, first_row, owned, 0)
    weight_sum = lax.dynamic_slice_in_dim(weight_sum, first_row, owned, 0)
    return (free_now, over, anchor, term_sum / weight_sum[:, None])


LOG2E = 1.4426950408889634
LIFT = 57.0
MESH = pl.DeviceIdType.MESH


def lanes_to_column(rows_form):
    parts = [
        jnp.broadcast_to(rows_form[r : r + 1, :], (128, 128)).T for r in range(rows_form.shape[0])
    ]
    return jnp.concatenate(parts, axis=0)


def split(x):
    high = x.astype(jnp.bfloat16)
    rest = x - high.astype(jnp.float32)
    middle = rest.astype(jnp.bfloat16)
    low = (rest - middle.astype(jnp.float32)).astype(jnp.bfloat16)
    return high, middle, low


def mbar_kernel(
    n,
    groups,
    terms_ref,
    coef_ref,
    counts_ref,
    labels_ref,
    start_ref,
    free_ref,
    over_ref,
    anchor_ref,
    means_ref,
    ok_ref,
    q_ref,
    t_ref,
    a_ref,
    w_ref,
    d_ref,
    acc_ref,
    inv_ref,
    x_ref,
    left_ref,
    right_ref,
    comm_ref,
    flag_ref,
    big_ref,
    half_ref,
    red_ref,
    got_ref,
    load_sem,
    send_sem,
    recv_sem,
    flag_send,
    flag_recv,
    half_sem,
    out_send,
    out_recv,
):
    f32, bf16 = jnp.float32, jnp.bfloat16
    group = lax.axis_index("groups")
    me = lax.axis_index("samples")
    blocks, states, wq = q_ref.shape
    rows = blocks * wq
    terms = t_ref.shape[0]
    owned = states // n
    chunks = load_sem.shape[0]
    chunk = rows // chunks

    def load(c):
        cols = pl.ds(pl.multiple_of(c * chunk, chunk), chunk)
        return pltpu.make_async_copy(terms_ref.at[:, cols], t_ref.at[:, cols], load_sem.at[c])

    barrier = pltpu.get_barrier_semaphore()
    for d in range(1, n):
        pl.semaphore_signal(
            barrier, inc=1, device_id=(group, lax.rem(me + d, n)), device_id_type=MESH
        )
    for d in range(1, groups):
        pl.semaphore_signal(
            barrier, inc=1, device_id=(lax.rem(group + d, groups), me), device_id_type=MESH
        )
    for c in range(chunks):
        load(c).start()

    ch, cm, cl = (p.astype(f32) for p in split(coef_ref[...] * (-LOG2E)))
    a_ref[...] = jnp.concatenate([ch, ch, cm, cm, ch, cl], axis=0).T.astype(bf16)

    counts = counts_ref[...].astype(f32)
    log_counts = jnp.log(counts)
    tiny = 1e-15
    most = 1e10

    def state_weights(free):
        shifted = log_counts + free
        top = jnp.max(jnp.max(shifted, axis=1, keepdims=True), axis=0, keepdims=True)
        return jnp.exp(shifted - top), top

    def gather_sums(block, count):
        lanes = [(c, j) for c in range(count) for j in range(0, wq, 128)]

        def tile(k, c, j):
            return q_ref[block + c, k : k + 8, j : j + 128]

        s = None
        for k in range(0, states, 8):
            w = w_ref[k : k + 8, :]
            p = [tile(k, c, j) * w for c, j in lanes]
            s = p if s is None else [x + y for x, y in zip(s, p)]
        inv = [1.0 / jnp.sum(x, axis=0, keepdims=True) for x in s]
        peak = functools.reduce(jnp.maximum, inv)
        inv_ref[...] = jnp.maximum(inv_ref[...], peak)
        wide = [jnp.broadcast_to(x, (8, 128)) for x in inv]
        for k in range(0, states, 8):
            t = [tile(k, c, j) * wide[i] for i, (c, j) in enumerate(lanes)]
            while len(t) > 1:
                t = [t[i] + t[i + 1] for i in range(0, len(t), 2)]
            acc_ref[k : k + 8, :] += t[0]

    def clear():
        acc_ref[...] = jnp.zeros_like(acc_ref)
        inv_ref[...] = jnp.zeros_like(inv_ref)

    weights, _ = state_weights(start_ref[...])
    w_ref[...] = lanes_to_column(weights)
    clear()

    def energies_of(b):
        cols = pl.multiple_of(b * wq, wq)
        th, tm, tl = split(t_ref[:, pl.ds(cols, wq)])
        stacked = jnp.concatenate([th, tm, th, tm, tl, th], axis=0)
        return jnp.dot(a_ref[...], stacked, preferred_element_type=f32)

    def energy_block(i, carry):
        b = i * 2
        es = [energies_of(b), energies_of(b + 1)]
        for c, e in enumerate(es):
            top = jnp.max(e, axis=0, keepdims=True) - LIFT
            q_ref[b + c] = jnp.exp2(e - top)
        gather_sums(b, 2)
        return carry

    def energy_chunk(c, carry):
        load(c).wait()
        per = chunk // (2 * wq)
        lax.fori_loop(c * per, (c + 1) * per, energy_block, 0)
        return carry

    lax.fori_loop(0, chunks, energy_chunk, 0)
    pl.semaphore_wait(barrier, n - 1 + groups - 1)

    good = counts > 0.0
    free = None
    for it in range(ITERS):
        if it:
            clear()

            def pass_block(b, carry):
                gather_sums(b * 2, 2)
                return carry

            lax.fori_loop(0, blocks // 2, pass_block, 0)
        sums = jnp.sum(acc_ref[...].T, axis=0, keepdims=True)
        halves = [sums[:, r : r + 128] for r in range(0, states, 128)]
        pad = comm_ref.shape[2] - len(halves)
        comm_ref[it, me] = jnp.concatenate(halves + [inv_ref[...]] * pad, axis=0)
        copies = []
        for d in range(1, n):
            copy = pltpu.make_async_remote_copy(
                src_ref=comm_ref.at[it, me],
                dst_ref=comm_ref.at[it, me],
                send_sem=send_sem.at[it, d],
                recv_sem=recv_sem.at[it, d],
                device_id=(group, lax.rem(me + d, n)),
                device_id_type=MESH,
            )
            copy.start()
            copies.append(copy)
        for copy in copies:
            copy.wait()
        everyone = comm_ref[it]
        total = jnp.sum(everyone[:, : states // 128], axis=0)
        peak = jnp.max(jnp.max(everyone, axis=0)[states // 128 :], axis=0, keepdims=True)
        peak = jnp.max(peak, axis=1, keepdims=True)
        good = good & (total >= tiny) & (peak <= most)
        logs = jnp.log(total)
        free = logs[0:1, 0:1] - logs
        before = weights
        weights, top = state_weights(free)
        w_ref[...] = lanes_to_column(weights)
    free_ref[...] = free

    change = weights / before
    least = jnp.min(jnp.min(change, axis=1, keepdims=True), axis=0, keepdims=True)
    widest = jnp.max(jnp.max(change, axis=1, keepdims=True), axis=0, keepdims=True)
    good = good & (weights >= 1e-30) & (peak <= most * least) & (total >= tiny * widest)
    good = jnp.min(jnp.where(good, 1.0, 0.0), axis=0, keepdims=True)
    good = jnp.broadcast_to(jnp.min(good, axis=1, keepdims=True), (8, 128))
    flag_ref[group] = good
    flags = []
    for d in range(1, groups):
        copy = pltpu.make_async_remote_copy(
            src_ref=flag_ref.at[group],
            dst_ref=flag_ref.at[group],
            send_sem=flag_send.at[d],
            recv_sem=flag_recv.at[d],
            device_id=(lax.rem(group + d, groups), me),
            device_id_type=MESH,
        )
        copy.start()
        flags.append(copy)

    d_ref[...] = lanes_to_column(jnp.exp(free - top))
    left_ref[...] = jnp.zeros_like(left_ref)
    right_ref[...] = jnp.zeros_like(right_ref)
    wd = x_ref.shape[1]
    sub = wq
    base = 3 * states
    x_ref[base + terms : base + terms + 16, :] = jnp.ones((16, wd), bf16)

    def weights_block(b, carry):
        cols = pl.multiple_of(b * wd, wd)
        for u in range(wd // sub):
            o = u * sub
            at = b * (wd // sub) + u
            s = None
            for k in range(0, states, 8):
                w = w_ref[k : k + 8, :]
                p = [q_ref[at, k : k + 8, j : j + 128] * w for j in range(0, sub, 128)]
                s = p if s is None else [x + y for x, y in zip(s, p)]
            inv = [1.0 / jnp.sum(x, axis=0, keepdims=True) for x in s]
            wide = [jnp.broadcast_to(x, (16, 128)) for x in inv]
            names = [
                jnp.broadcast_to(labels_ref[:, pl.ds(cols + o + j, 128)], (16, 128))
                for j in range(0, sub, 128)
            ]
            ids = lax.broadcasted_iota(jnp.int32, (16, 128), 0)
            for k in range(0, states, 16):
                scale = d_ref[k : k + 16, :]
                for i, j in enumerate(range(0, sub, 128)):
                    v = q_ref[at, k : k + 16, j : j + 128] * wide[i] * scale
                    high = v.astype(bf16)
                    x_ref[k : k + 16, o + j : o + j + 128] = high
                    x_ref[states + k : states + k + 16, o + j : o + j + 128] = (
                        v - high.astype(f32)
                    ).astype(bf16)
                    x_ref[2 * states + k : 2 * states + k + 16, o + j : o + j + 128] = jnp.where(
                        names[i] == ids + k, 1.0, 0.0
                    ).astype(bf16)
            t = t_ref[:, pl.ds(cols + o, sub)]
            th = t.astype(bf16)
            x_ref[base : base + terms, o : o + sub] = th
            x_ref[base + terms + 16 : base + 2 * terms + 16, o : o + sub] = (
                t - th.astype(f32)
            ).astype(bf16)
        nt = (((1,), (1,)), ((), ()))
        left_ref[...] += lax.dot_general(
            x_ref[...], x_ref[0:states, :], nt, preferred_element_type=f32
        )
        right_ref[...] += lax.dot_general(
            x_ref[2 * states : base + terms + 16, :],
            x_ref[states : 2 * states, :],
            nt,
            preferred_element_type=f32,
        )
        return carry

    lax.fori_loop(0, rows // wd, weights_block, 0)

    cross = left_ref[states : 2 * states, :]
    over = left_ref[0:states, :] + cross + cross.T
    anchor = left_ref[2 * states : base, :] + right_ref[0:states, :]
    sums = (
        left_ref[base : base + terms, :]
        + left_ref[base + terms + 16 : base + 2 * terms + 16, :]
        + right_ref[states : states + terms, :]
    )
    mass = left_ref[base + terms : base + terms + 16, :] + right_ref[
        states + terms : states + terms + 16, :
    ]
    fill = jnp.zeros((128 - terms - 16, states), f32)
    sums = jnp.concatenate([sums, mass, fill], axis=0).T
    for p in range(n):
        own = slice(p * owned, (p + 1) * owned)
        big_ref[p % 2, p // 2, :, 0:states] = over[own]
        big_ref[p % 2, p // 2, :, states : 2 * states] = anchor[own]
        big_ref[p % 2, p // 2, :, 2 * states :] = sums[own]

    side = lax.rem(me, 2)
    place = me // 2
    pair = pltpu.make_async_remote_copy(
        src_ref=big_ref.at[1 - side],
        dst_ref=half_ref,
        send_sem=half_sem.at[0],
        recv_sem=half_sem.at[1],
        device_id=(group, place * 2 + 1 - side),
        device_id_type=MESH,
    )
    pair.start()
    pair.wait()
    red_ref[...] = big_ref[side] + half_ref[...]
    copies = []
    for d in range(1, n // 2):
        there = lax.rem(place + d, n // 2)
        copy = pltpu.make_async_remote_copy(
            src_ref=red_ref.at[there],
            dst_ref=got_ref.at[place],
            send_sem=out_send.at[d],
            recv_sem=out_recv.at[d],
            device_id=(group, there * 2 + side),
            device_id_type=MESH,
        )
        copy.start()
        copies.append(copy)
    got_ref[place] = red_ref[place]
    for copy in copies:
        copy.wait()
    for copy in flags:
        copy.wait()
    ok_ref[...] = jnp.min(flag_ref[...], axis=0)
    final = jnp.sum(got_ref[...], axis=0)
    wide_counts = jnp.concatenate([counts[r : r + 1] for r in range(states // 128)], axis=1)
    over_ref[...] = final[:, 0:states] * wide_counts
    anchor_ref[...] = final[:, states : 2 * states]
    tail = final[:, 2 * states :]
    means_ref[...] = tail[:, 0:terms] / tail[:, terms : terms + 1]


WIDTH_Q = 512
WIDTH_D = 2048


def local(n, groups, terms, coefficients, counts, labels, f_start):
    rows, width = terms.shape
    states = coefficients.shape[1]
    f32, bf16 = jnp.float32, jnp.bfloat16
    owned = states // n
    chunks = 8
    vmem = pl.BlockSpec(memory_space=pltpu.VMEM)
    stacked = 3 * states + 2 * width + 16
    block = (n // 2, owned, 2 * states + 128)
    dma = pltpu.SemaphoreType.DMA
    free, over, anchor, means, ok = pl.pallas_call(
        functools.partial(mbar_kernel, n, groups),
        out_shape=(
            jax.ShapeDtypeStruct((states // 128, 128), f32),
            jax.ShapeDtypeStruct((owned, states), f32),
            jax.ShapeDtypeStruct((owned, states), f32),
            jax.ShapeDtypeStruct((owned, width), f32),
            jax.ShapeDtypeStruct((8, 128), f32),
        ),
        in_specs=[pl.BlockSpec(memory_space=pltpu.HBM), vmem, vmem, vmem, vmem],
        out_specs=(vmem,) * 5,
        scratch_shapes=[
            pltpu.VMEM((rows // WIDTH_Q, states, WIDTH_Q), f32),
            pltpu.VMEM((width, rows), f32),
            pltpu.VMEM((states, 6 * width), bf16),
            pltpu.VMEM((states, 128), f32),
            pltpu.VMEM((states, 128), f32),
            pltpu.VMEM((states, 128), f32),
            pltpu.VMEM((1, 128), f32),
            pltpu.VMEM((stacked, WIDTH_D), bf16),
            pltpu.VMEM((stacked, states), f32),
            pltpu.VMEM((states + width + 16, states), f32),
            pltpu.VMEM((ITERS, n, 4, 128), f32),
            pltpu.VMEM((groups, 8, 128), f32),
            pltpu.VMEM((2,) + block, f32),
            pltpu.VMEM(block, f32),
            pltpu.VMEM(block, f32),
            pltpu.VMEM(block, f32),
            dma((chunks,)),
            dma((ITERS, n)),
            dma((ITERS, n)),
            dma((groups,)),
            dma((groups,)),
            dma((2,)),
            dma((n // 2,)),
            dma((n // 2,)),
        ],
        compiler_params=pltpu.CompilerParams(
            collective_id=0, has_side_effects=True, vmem_limit_bytes=62 * 1024 * 1024
        ),
    )(
        terms.T,
        coefficients,
        counts.reshape(states // 128, 128),
        labels.reshape(1, rows),
        f_start.reshape(states // 128, 128),
    )
    fast = (free.reshape(states), over, anchor, means)
    return lax.cond(
        ok[0, 0] > 0.5,
        lambda: fast,
        lambda: general(terms, coefficients, counts, labels, f_start),
    )


def solution(mesh):
    return jax.shard_map(
        functools.partial(local, mesh.shape["samples"], mesh.shape["groups"]),
        mesh=mesh,
        in_specs=(
            P(("groups", "samples"), None),
            P(),
            P("groups"),
            P(("groups", "samples")),
            P("groups"),
        ),
        out_specs=(
            P("groups"),
            P(("groups", "samples"), None),
            P(("groups", "samples"), None),
            P(("groups", "samples"), None),
        ),
        check_vma=False,
    )
```
